32 devices in a mesh: fsdp: 8 (over y, x, core), ctx: 4 (over z).
Axes of the slice: x: 2, y: 2, z: 4, core: 2. Of those that a mesh axis runs over, the one named last changes fastest.
Arguments:
- tokens: bfloat16 [4096, 8192], P('fsdp'), may hold values from -12 to 12
- wq: bfloat16 [8192, 4096], P('fsdp', 'ctx'), may hold values from -0.0625 to 0.0625
- wo: bfloat16 [4096, 8192], P('ctx', 'fsdp'), may hold values from -1.5 to 1.5
- key_cache: bfloat16 [8192, 1024], P(('fsdp', 'ctx')), may hold values from -500 to 500, as said below
- value_cache: bfloat16 [8192, 1024], P(('fsdp', 'ctx')), may hold values from -6 to 6
- key_blocks: int32 [8, 4, 8], P('fsdp'), may hold values from 0 to 7, as said below
Outputs:
- mixed: bfloat16 [4096, 8192], P('fsdp', 'ctx')
The draws below stay inside these ranges and needn't reach their ends.
Inputs may be any that keep to these rules, and one draw needn't show every extreme that they name: `key_cache`: keys of order one; a sequence's first block may hold much larger ones. `key_blocks`: for query block b of sequence s, entries 0 to 2 name key blocks 8 - 4 + b - 2, 4 + b - 1 and 4 + b; entries 3 and 4 name blocks 0 and 1; the last 3 entries are random blocks. Counting the random entries of a sequence over its query blocks in order as t = 0, 1, ..., the t-th lies in blocks k * 2 to (k+1) * 2 - 1 with k = 1 + t mod (2); entries may repeat.
All inputs are finite; a program needn't handle non-finite values.
Results may differ from the reference program's by a relative error of at most 0.018.
Values may be sent and summed in bfloat16 or wider, within the bound.
A program may use at most 128 MiB of HBM per device.

```python
import jax
import jax.numpy as jnp
from jax import lax

D = 8192
HEADS = 32
KV_HEADS = 8
HEAD = 128
BLOCK = 128
QB = 4
RANDS = 3
BLK_DEV = 2
Q_LEN = 512
CACHE_BLOCKS = 8
KEYS = 1024
SEQS = 8
ROWS = 4096
N_CTX = 4


def draw_tokens(key, part):
    base = jnp.clip(jax.random.normal(key, (ROWS, D), jnp.float32), -6.0, 6.0)
    return base.astype(jnp.bfloat16)


def draw_key_cache(key, part):
    width = KV_HEADS * HEAD
    base = jnp.clip(jax.random.normal(key, (SEQS, KEYS, width), jnp.float32), -6.0, 6.0)
    return base.reshape(SEQS * KEYS, width).astype(jnp.bfloat16)


def draw_key_blocks(key, part):
    owner_count = CACHE_BLOCKS // BLK_DEV
    query_ids = jnp.arange(QB, dtype=jnp.int32)
    own_ids = CACHE_BLOCKS - QB + query_ids
    window = own_ids[:, None] + jnp.arange(-2, 1, dtype=jnp.int32)[None, :]
    anchors = jnp.broadcast_to(jnp.arange(2, dtype=jnp.int32)[None, :], (QB, 2))
    entry_ids = jnp.arange(QB * RANDS, dtype=jnp.int32).reshape(QB, RANDS)
    owner_ids = 1 + entry_ids % (owner_count - 2)
    offsets = jax.random.randint(key, (SEQS, QB, RANDS), 0, BLK_DEV, dtype=jnp.int32)
    randoms = owner_ids[None, :, :] * BLK_DEV + offsets
    fixed_part = jnp.concatenate([window, anchors], axis=1)
    listed = jnp.concatenate([jnp.broadcast_to(fixed_part[None, :, :], (SEQS, QB, 5)), randoms], axis=2)
    return listed.astype(jnp.int32)


def levels(stream_key, dims, cuts, least, high):
    def one(position, shards_of):
        draws = jax.random.uniform(jax.random.fold_in(jax.random.fold_in(stream_key, 6), position), (shards_of,), jnp.float32, least / len(cuts), high / len(cuts))
        return jnp.repeat(jnp.exp(draws), dims[position] // shards_of).reshape((-1,) + (1,) * (len(dims) - position - 1))

    gain = one(*cuts[0])
    for cut in cuts[1:]:
        gain = gain * one(*cut)
    return gain


def bell_draw(stream_key, dims, scale, limit, shards=(), held_as=jnp.bfloat16):
    gain = levels(stream_key, dims, shards, -0.22, 0.18) if shards else 1.0
    entries = jax.random.normal(stream_key, dims, jnp.float32) * scale * gain
    return jnp.minimum(jnp.maximum(entries, -limit), limit).astype(held_as)


def setup_inputs(seed: int = 0) -> dict:
    key_list = jax.random.split(jax.random.key(seed), 7)
    return {
        "tokens": draw_tokens(jax.random.fold_in(key_list[6], 71), 0),
        "wq": bell_draw(key_list[1], (D, HEADS * HEAD), D ** -0.5, 0.0625, ((0, 8), (1, 4))),
        "wo": bell_draw(key_list[2], (HEADS * HEAD, D), (HEAD // 8) ** -0.5, 1.5, ((0, 4), (1, 8))),
        "key_cache": draw_key_cache(jax.random.fold_in(key_list[6], 71), 0),
        "value_cache": bell_draw(key_list[4], (SEQS * KEYS, KV_HEADS * HEAD), 1.0, 6.0, ((0, 32),)),
        "key_blocks": draw_key_blocks(jax.random.fold_in(key_list[6], 71), 0),
    }


rope_base = 1000000.0


def rotate(vectors, positions):
    half_width = vectors.shape[-1] // 2
    frequency = rope_base ** (-(jnp.arange(half_width, dtype=jnp.float32) * 2.0) / vectors.shape[-1])
    angles = positions.astype(jnp.float32)[:, None] * frequency[None, :]
    cosine_table = jnp.cos(angles)[:, None, :]
    sine_table = jnp.sin(angles)[:, None, :]
    front_half = vectors[..., :half_width]
    back_half = vectors[..., half_width:]
    return jnp.concatenate([front_half * cosine_table - back_half * sine_table, back_half * cosine_table + front_half * sine_table], axis=-1)


def reference(tokens, wq, wo, key_cache, value_cache, key_blocks):
    group_size = HEADS // KV_HEADS
    positions = (KEYS - Q_LEN) + jnp.arange(Q_LEN, dtype=jnp.int32)
    projected = jnp.dot(tokens, wq, preferred_element_type=jnp.float32).reshape(SEQS, Q_LEN, HEADS, HEAD)
    query = (rotate(projected, positions) * (HEAD ** -0.5)).astype(jnp.bfloat16)
    keys = key_cache.reshape(SEQS, KEYS // BLOCK, BLOCK, KV_HEADS, HEAD)
    values = value_cache.reshape(SEQS, KEYS // BLOCK, BLOCK, KV_HEADS, HEAD)
    own_block = (KEYS - Q_LEN) // BLOCK + jnp.arange(QB, dtype=jnp.int32)
    causal = jnp.arange(BLOCK)[None, :] <= jnp.arange(BLOCK)[:, None]

    def one_sequence(items):
        query_seq, keys_seq, values_seq, lists = items
        picked_keys = jnp.take(keys_seq, lists, axis=0).astype(jnp.float32)
        picked_values = jnp.take(values_seq, lists, axis=0).astype(jnp.float32)
        shaped = query_seq.reshape(QB, BLOCK, KV_HEADS, group_size, HEAD).astype(jnp.float32)
        scores = jnp.einsum("bqkgd,bnskd->bkgqns", shaped, picked_keys)
        own = lists == own_block[:, None]
        allowed = jnp.logical_or(jnp.logical_not(own)[:, None, None, None, :, None], causal[None, None, None, :, None, :])
        scores = jnp.where(allowed, scores, -jnp.inf)
        top_score = jnp.max(scores, axis=(4, 5), keepdims=True)
        raised = jnp.exp(scores - top_score)
        weights = (raised / jnp.sum(raised, axis=(4, 5), keepdims=True)).astype(jnp.bfloat16)
        context = jnp.einsum("bkgqns,bnskd->bqkgd", weights.astype(jnp.float32), picked_values)
        return context.astype(jnp.bfloat16).reshape(Q_LEN, HEADS * HEAD)

    contexts = lax.map(one_sequence, (query, keys, values, key_blocks)).reshape(ROWS, HEADS * HEAD)
    group_cols = (HEADS // N_CTX) * HEAD
    total = jnp.zeros((ROWS, D), jnp.float32)
    for index in range(N_CTX):
        share_sum = jnp.dot(contexts[:, index * group_cols:(index + 1) * group_cols], wo[index * group_cols:(index + 1) * group_cols], preferred_element_type=jnp.float32).astype(jnp.bfloat16)
        share_sum = lax.optimization_barrier(share_sum)
        total = total + share_sum.astype(jnp.float32)
    return total.astype(jnp.bfloat16)
```

```python
import functools

import jax
import jax.numpy as jnp
from jax import lax
from jax.experimental import pallas as pl
from jax.experimental.pallas import tpu as pltpu
from jax.sharding import PartitionSpec as P

HEAD = 128
BLOCK = 128
LANES = 128
MESH = pl.DeviceIdType.MESH

rope_base = 1000000.0


def tables(row_count, key_total):
    half_width = HEAD // 2
    frequency = rope_base ** (-(jnp.arange(half_width, dtype=jnp.float32) * 2.0) / HEAD)
    positions = key_total - row_count + jnp.arange(row_count, dtype=jnp.int32)
    angles = positions.astype(jnp.float32)[:, None] * frequency[None, :]
    cosine = jnp.cos(angles) * HEAD ** (-0.5)
    sine = jnp.sin(angles) * HEAD ** (-0.5)
    return jnp.concatenate([cosine, cosine], axis=1), jnp.concatenate([-sine, sine], axis=1)


def low_bit(m):
    return m & -m


def high_bit(m):
    return 1 << (m.bit_length() - 1)


def route(mask, piece):
    return low_bit(mask) if piece % 2 == 0 else high_bit(mask)


def kernel(
    cfg,
    lists, tokens, wq, wo, kc, vc, cos_ref, sin_ref,
    out,
    tok, wq_buf, wo_buf, k_buf, v_buf, acc, qc, k_pick, v_pick, bias, recv_main, recv_dn,
    tok_sem, own_sem, send_sem, wq_sem, wo_sem, kv_send, kv_sem, rs_send, rs_sem, dn_sem, out_sem,
):
    n_f, n_c, nq, nw = cfg
    chips = n_f // 2
    bits = [1 << i for i in range(chips.bit_length() - 1)]
    masks = sorted(range(1, chips), key=lambda m: (bin(m).count("1"), m))
    f = lax.axis_index("fsdp")
    c = lax.axis_index("ctx")
    rows = tok.shape[1]
    depth = tok.shape[2]
    qcols = wq_buf.shape[2]
    qp = wq_buf.shape[1] // nq
    wp = depth // nw
    ratio = n_f // n_c
    blk_dev = kc.shape[0]
    kv_cols = k_buf.shape[2]
    kv_local = kv_cols // HEAD
    group = qcols // kv_cols
    n_blocks = k_buf.shape[0]
    q_blocks = rows // BLOCK
    n_list = lists.shape[2]

    def flip(x):
        bit, total = 1, 0
        while bit < n_f:
            total += lax.rem(lax.div(f, bit) + x // bit, 2) * bit
            bit *= 2
        return total

    def peer(x):
        return (flip(x), c)

    barrier = pltpu.get_barrier_semaphore()
    for x in [1] + [2 * b for b in bits]:
        pl.semaphore_signal(barrier, inc=1, device_id=peer(x), device_id_type=MESH)
    for d in range(1, n_c):
        pl.semaphore_signal(
            barrier, inc=1, device_id=(f, lax.rem(c + d, n_c)), device_id_type=MESH
        )
    pl.semaphore_wait(barrier, 1 + len(bits) + n_c - 1)

    sent = []

    def view(kind, ref, s):
        if kind == 0:
            return ref.at[pl.ds(s * qp, qp), :]
        return ref.at[:, pl.ds(s * wp, wp)]

    shard = (wq, wo)
    bufs = (wq_buf, wo_buf)
    sems = (wq_sem, wo_sem)
    counts = (nq, nw)

    def send(kind, src, slot, s, to):
        copy = pltpu.make_async_remote_copy(
            src_ref=src,
            dst_ref=view(kind, bufs[kind].at[slot], s),
            send_sem=send_sem.at[len(sent)],
            recv_sem=sems[kind].at[slot, s],
            device_id=peer(to),
            device_id_type=MESH,
        )
        copy.start()
        sent.append(copy)

    def arrived(kind, slot, s):
        pltpu.make_async_remote_copy(
            src_ref=view(kind, bufs[kind].at[slot], s),
            dst_ref=view(kind, bufs[kind].at[slot], s),
            send_sem=send_sem.at[0],
            recv_sem=sems[kind].at[slot, s],
            device_id=peer(1),
            device_id_type=MESH,
        ).wait_recv()

    stream = [(0, s) for s in range(nq)] + [(1, s) for s in range(nw)]

    def directs(i):
        if i < len(stream):
            kind, s = stream[i]
            for b in bits:
                send(kind, view(kind, shard[kind], s), 2 * b, s, 2 * b)

    def kv_copy(which, d):
        other = lax.rem(c + d, n_c)
        src, dst = ((kc, k_buf), (vc, v_buf))[which]
        return pltpu.make_async_remote_copy(
            src_ref=src.at[:, :, pl.ds(pl.multiple_of(other * kv_cols, LANES), kv_cols)],
            dst_ref=dst.at[pl.ds(c * blk_dev, blk_dev)],
            send_sem=kv_send.at[which, d],
            recv_sem=kv_sem.at[which, d],
            device_id=(f, other),
            device_id_type=MESH,
        )

    directs(0)
    for s in range(nq):
        send(0, view(0, wq, s), 1, s, 1)
    directs(1)

    def tok_copy(j):
        start = pl.multiple_of(flip(j) * depth, LANES)
        return pltpu.make_async_copy(tokens.at[:, pl.ds(start, depth)], tok.at[j], tok_sem.at[j])

    own_q = pltpu.make_async_copy(wq, wq_buf.at[0], own_sem.at[0])
    own_q.start()
    for j in range(n_f):
        tok_copy(j).start()
    kv_sent = []
    for d in range(1, n_c):
        for which in range(2):
            copy = kv_copy(which, d)
            copy.start()
            kv_sent.append(copy)
    mine = pl.ds(pl.multiple_of(c * kv_cols, LANES), kv_cols)
    own_k = pltpu.make_async_copy(kc.at[:, :, mine], k_buf.at[pl.ds(c * blk_dev, blk_dev)], own_sem.at[2])
    own_v = pltpu.make_async_copy(vc.at[:, :, mine], v_buf.at[pl.ds(c * blk_dev, blk_dev)], own_sem.at[3])
    own_k.start()
    own_v.start()
    own_o = pltpu.make_async_copy(wo, wo_buf.at[0], own_sem.at[1])
    own_o.start()
    for s in range(nw):
        send(1, view(1, wo, s), 1, s, 1)

    acc[...] = jnp.zeros_like(acc)
    tile = min(256, qcols)
    tiles = qcols // tile

    def q_piece(j, s):
        left = tok[j, :, s * qp:(s + 1) * qp]

        @pl.loop(0, tiles)
        def _(t):
            cols = pl.ds(pl.multiple_of(t * tile, tile), tile)
            acc[:, cols] += jnp.dot(
                left, wq_buf[j, s * qp:(s + 1) * qp, cols], preferred_element_type=jnp.float32
            )

    def q_whole(j):
        @pl.loop(0, tiles)
        def _(t):
            cols = pl.ds(pl.multiple_of(t * tile, tile), tile)
            acc[:, cols] += jnp.dot(tok[j], wq_buf[j, :, cols], preferred_element_type=jnp.float32)

    own_q.wait()
    for j in range(n_f):
        tok_copy(j).wait()
    for s in range(nq):
        arrived(0, 1, s)

    @pl.loop(0, 2)
    def _(j):
        q_whole(j)

    def pass_on(i):
        kind, s = stream[i]
        for m in masks:
            arrived(kind, 2 * m, s)
            piece = view(kind, bufs[kind].at[2 * m], s)
            for b in bits:
                if not (m & b) and route(m | b, s) == b:
                    send(kind, piece, 2 * (m | b), s, 2 * b)
            send(kind, piece, 2 * m + 1, s, 1)
            if m == bits[-1]:
                directs(i + 2)

    for s in range(nq):
        pass_on(s)

        @pl.loop(2, n_f)
        def _(j):
            @pl.when(lax.rem(j, 2) == 1)
            def _():
                arrived(0, j, s)

            q_piece(j, s)

    for h in range(qcols // HEAD):
        cols = slice(h * HEAD, (h + 1) * HEAD)
        x = acc[:, cols]
        turned = x * cos_ref[...] + pltpu.roll(x, HEAD // 2, 1) * sin_ref[...]
        qc[:, cols] = turned.astype(jnp.bfloat16)

    own_k.wait()
    own_v.wait()
    for copy in kv_sent:
        copy.wait_recv()

    @pl.loop(0, q_blocks)
    def _(b):
        q_rows = pl.ds(pl.multiple_of(b * BLOCK, BLOCK), BLOCK)
        own_block = n_blocks - q_blocks + b
        later = lax.broadcasted_iota(jnp.int32, (BLOCK, BLOCK), 1) > lax.broadcasted_iota(
            jnp.int32, (BLOCK, BLOCK), 0
        )
        for n in range(n_list):
            entry = lists[0, b, n]
            hide = jnp.where(entry == own_block, -jnp.inf, 0.0)
            bias[:, n * BLOCK:(n + 1) * BLOCK] = jnp.where(later, hide, 0.0)
        for g in range(kv_local):
            head_cols = slice(g * HEAD, (g + 1) * HEAD)
            for n in range(n_list):
                entry = lists[0, b, n]
                k_pick[n * BLOCK:(n + 1) * BLOCK, :] = k_buf[entry, :, head_cols]
                v_pick[n * BLOCK:(n + 1) * BLOCK, :] = v_buf[entry, :, head_cols]
            for i in range(group):
                h = g * group + i
                cols = slice(h * HEAD, (h + 1) * HEAD)
                scores = lax.dot_general(
                    qc[q_rows, cols], k_pick[...], (((1,), (1,)), ((), ())),
                    preferred_element_type=jnp.float32,
                ) + bias[...]
                top = jnp.max(scores, axis=1, keepdims=True)
                raised = jnp.exp(scores - top)
                total = jnp.sum(raised, axis=1, keepdims=True)
                mixed = jnp.dot(
                    raised.astype(jnp.bfloat16), v_pick[...], preferred_element_type=jnp.float32
                )
                qc[q_rows, cols] = (mixed / total).astype(jnp.bfloat16)

    last = n_c - 1

    def place(j):
        target = flip(j)
        return lax.div(target, ratio), lax.rem(target, ratio)

    def rs_copy(j, s, to_dn):
        dst, part = place(j)
        cols = pl.ds(s * wp, wp)
        nxt = jnp.where(c < dst, c + 1, c - 1)
        return pltpu.make_async_remote_copy(
            src_ref=tok.at[j, :, cols],
            dst_ref=recv_dn.at[part, :, cols] if to_dn else recv_main.at[j, :, cols],
            send_sem=rs_send.at[j, s],
            recv_sem=dn_sem.at[part, s] if to_dn else rs_sem.at[j, s],
            device_id=(f, nxt),
            device_id_type=MESH,
        )

    def rs_start(j, s):
        dst, _ = place(j)

        @pl.when(c == dst + 1)
        def _():
            rs_copy(j, s, True).start()

        @pl.when(c != dst + 1)
        def _():
            rs_copy(j, s, False).start()

    def share(j, s):
        cols = slice(s * wp, (s + 1) * wp)
        tok[j, :, cols] = jnp.dot(
            qc[...], wo_buf[j, :, cols], preferred_element_type=jnp.float32
        ).astype(jnp.bfloat16)
        dst, _ = place(j)

        @pl.when(jnp.logical_and(c != dst, jnp.logical_or(c == 0, c == last)))
        def _():
            rs_start(j, s)

    def out_copy(j, s):
        _, part = place(j)
        start = pl.multiple_of(part * depth + s * wp, LANES)
        return pltpu.make_async_copy(
            tok.at[j, :, pl.ds(s * wp, wp)], out.at[:, pl.ds(start, wp)], out_sem.at[part, s]
        )

    def progress(j, s):
        dst, part = place(j)
        cols = slice(s * wp, (s + 1) * wp)
        middle = jnp.logical_and(c > 0, c < last)
        is_dst = c == dst

        def f32(x):
            return x.astype(jnp.float32)

        @pl.when(jnp.logical_and(middle, jnp.logical_not(is_dst)))
        def _():
            rs_copy(j, s, False).wait_recv()
            tok[j, :, cols] = (f32(tok[j, :, cols]) + f32(recv_main[j, :, cols])).astype(jnp.bfloat16)
            rs_start(j, s)

        @pl.when(is_dst)
        def _():
            @pl.when(c > 0)
            def _():
                rs_copy(j, s, False).wait_recv()

            @pl.when(c < last)
            def _():
                rs_copy(j, s, True).wait_recv()

            @pl.when(c == 0)
            def _():
                tok[j, :, cols] = (f32(tok[j, :, cols]) + f32(recv_dn[part, :, cols])).astype(jnp.bfloat16)

            @pl.when(c == last)
            def _():
                tok[j, :, cols] = (f32(tok[j, :, cols]) + f32(recv_main[j, :, cols])).astype(jnp.bfloat16)

            @pl.when(middle)
            def _():
                tok[j, :, cols] = (
                    f32(tok[j, :, cols]) + f32(recv_main[j, :, cols]) + f32(recv_dn[part, :, cols])
                ).astype(jnp.bfloat16)

            out_copy(j, s).start()

    own_o.wait()
    for s in range(nw):
        arrived(1, 1, s)
    for s in range(nw):
        @pl.loop(0, 2)
        def _(j):
            share(j, s)

    for s in range(nw):
        pass_on(nq + s)

        @pl.loop(2, n_f)
        def _(j):
            @pl.when(lax.rem(j, 2) == 1)
            def _():
                arrived(1, j, s)

            share(j, s)

        if s == 0:
            for t in range(nw):
                @pl.loop(0, 2)
                def _(j):
                    progress(j, t)
        else:
            @pl.loop(2, n_f)
            def _(j):
                progress(j, s - 1)

    @pl.loop(2, n_f)
    def _(j):
        progress(j, nw - 1)

    assert len(sent) == send_sem.shape[0]
    for copy in sent + kv_sent:
        copy.wait_send()
    for s in range(nw):
        @pl.loop(0, n_f)
        def _(j):
            dst, _ = place(j)

            @pl.when(c == dst)
            def _():
                out_copy(j, s).wait()

            @pl.when(c != dst)
            def _():
                rs_copy(j, s, False).wait_send()


def body(n_f, n_c, tokens, wq, wo, key_cache, value_cache, key_blocks):
    rows, width = tokens.shape
    depth = width // n_f
    qcols = wq.shape[1]
    cache = key_cache.shape[0]
    blk_dev = cache // BLOCK
    kv_cols = key_cache.shape[1] // n_c
    n_list = key_blocks.shape[2]
    cosine, sine = tables(rows, cache * n_c)
    nq = max(1, min(4, wq.shape[0] // LANES))
    nw = max(1, min(4, wo.shape[1] // LANES))
    any_spec = pl.BlockSpec(memory_space=pl.ANY)
    vmem_spec = pl.BlockSpec(memory_space=pltpu.VMEM)
    ratio = n_f // n_c
    bf16 = jnp.bfloat16
    dma = pltpu.SemaphoreType.DMA
    return pl.pallas_call(
        functools.partial(kernel, (n_f, n_c, nq, nw)),
        out_shape=jax.ShapeDtypeStruct((rows, width // n_c), bf16),
        in_specs=[pl.BlockSpec(memory_space=pltpu.SMEM)] + [any_spec] * 5 + [vmem_spec] * 2,
        out_specs=any_spec,
        scratch_shapes=[
            pltpu.VMEM((n_f, rows, depth), bf16),
            pltpu.VMEM((n_f,) + wq.shape, bf16),
            pltpu.VMEM((n_f,) + wo.shape, bf16),
            pltpu.VMEM((blk_dev * n_c, BLOCK, kv_cols), bf16),
            pltpu.VMEM((blk_dev * n_c, BLOCK, kv_cols), bf16),
            pltpu.VMEM((rows, qcols), jnp.float32),
            pltpu.VMEM((rows, qcols), bf16),
            pltpu.VMEM((n_list * BLOCK, HEAD), bf16),
            pltpu.VMEM((n_list * BLOCK, HEAD), bf16),
            pltpu.VMEM((BLOCK, n_list * BLOCK), jnp.float32),
            pltpu.VMEM((n_f, rows, depth), bf16),
            pltpu.VMEM((ratio, rows, depth), bf16),
            dma((n_f,)),
            dma((4,)),
            dma(((nq + nw) * (n_f - 1),)),
            dma((n_f, nq)),
            dma((n_f, nw)),
            dma((2, n_c)),
            dma((2, n_c)),
            dma((n_f, nw)),
            dma((n_f, nw)),
            dma((ratio, nw)),
            dma((ratio, nw)),
        ],
        compiler_params=pltpu.CompilerParams(
            collective_id=0, has_side_effects=True, vmem_limit_bytes=67043328
        ),
    )(
        key_blocks,
        tokens,
        wq,
        wo,
        key_cache.reshape(blk_dev, BLOCK, key_cache.shape[1]),
        value_cache.reshape(blk_dev, BLOCK, value_cache.shape[1]),
        cosine,
        sine,
    )


def solution(mesh):
    in_specs = (
        P("fsdp", None),
        P("fsdp", "ctx"),
        P("ctx", "fsdp"),
        P(("fsdp", "ctx"), None),
        P(("fsdp", "ctx"), None),
        P("fsdp", None, None),
    )
    step = functools.partial(body, mesh.shape["fsdp"], mesh.shape["ctx"])
    return jax.shard_map(
        step, mesh=mesh, in_specs=in_specs, out_specs=P("fsdp", "ctx"), check_vma=False
    )
```

```python
import functools

import jax
import jax.numpy as jnp
from jax import lax
from jax.experimental import pallas as pl
from jax.experimental.pallas import tpu as pltpu
from jax.sharding import PartitionSpec as P

HEAD = 128
BLOCK = 128
LANES = 128
AHEAD = 2
MESH = pl.DeviceIdType.MESH

rope_base = 1000000.0


def tables(row_count, key_total):
    half_width = HEAD // 2
    frequency = rope_base ** (-(jnp.arange(half_width, dtype=jnp.float32) * 2.0) / HEAD)
    positions = key_total - row_count + jnp.arange(row_count, dtype=jnp.int32)
    angles = positions.astype(jnp.float32)[:, None] * frequency[None, :]
    cosine = jnp.cos(angles) * HEAD ** (-0.5)
    sine = jnp.sin(angles) * HEAD ** (-0.5)
    return jnp.concatenate([cosine, cosine], axis=1), jnp.concatenate([-sine, sine], axis=1)


def low_bit(m):
    return m & -m


def high_bit(m):
    return 1 << (m.bit_length() - 1)


def route(mask, piece):
    return low_bit(mask) if piece % 2 == 0 else high_bit(mask)


def kernel(
    cfg,
    lists, tokens, wq, wo, kc, vc, cos_ref, sin_ref,
    out,
    tok, wq_buf, wo_buf, k_buf, v_buf, acc, qc, k_pick, v_pick, bias, ctx_all, ctx_perm, staged,
    tok_sem, own_sem, send_sem, wq_sem, wo_sem, kv_send, kv_sem, ctx_send, ctx_sem,
    move_send, move_sem, out_sem,
):
    n_f, n_c, nq, nw = cfg
    chips = n_f // 2
    bits = [1 << i for i in range(chips.bit_length() - 1)]
    masks = sorted(range(1, chips), key=lambda m: (bin(m).count("1"), m))
    f = lax.axis_index("fsdp")
    c = lax.axis_index("ctx")
    rows = tok.shape[1]
    depth = tok.shape[2]
    qcols = wq_buf.shape[2]
    qp = wq_buf.shape[1] // nq
    wo_cols = wo.shape[1]
    wp = wo_buf.shape[2] // nw
    part = wo.shape[0] // chips
    ratio = n_f // n_c
    blk_dev = kc.shape[0]
    kv_cols = k_buf.shape[2]
    kv_local = kv_cols // HEAD
    group = qcols // kv_cols
    n_blocks = k_buf.shape[0]
    q_blocks = rows // BLOCK
    n_list = lists.shape[2]

    def flip(x):
        bit, total = 1, 0
        while bit < n_f:
            total += lax.rem(lax.div(f, bit) + x // bit, 2) * bit
            bit *= 2
        return total

    def peer(x):
        return (flip(x), c)

    barrier = pltpu.get_barrier_semaphore()
    me = f * n_c + c

    @pl.loop(1, n_f * n_c)
    def _(d):
        other = lax.rem(me + d, n_f * n_c)
        pl.semaphore_signal(
            barrier, inc=1, device_id=(lax.div(other, n_c), lax.rem(other, n_c)), device_id_type=MESH
        )

    pl.semaphore_wait(barrier, n_f * n_c - 1)

    sent = []

    def view(kind, ref, s):
        if kind == 0:
            return ref.at[pl.ds(s * qp, qp), :]
        return ref.at[:, pl.ds(s * wp, wp)]

    shard = (wq, wo_buf.at[0])
    bufs = (wq_buf, wo_buf)
    sems = (wq_sem, wo_sem)
    counts = (nq, nw)

    def send(kind, src, slot, s, to):
        copy = pltpu.make_async_remote_copy(
            src_ref=src,
            dst_ref=view(kind, bufs[kind].at[slot], s),
            send_sem=send_sem.at[len(sent)],
            recv_sem=sems[kind].at[slot, s],
            device_id=peer(to),
            device_id_type=MESH,
        )
        copy.start()
        sent.append(copy)

    def arrived(kind, slot, s):
        pltpu.make_async_remote_copy(
            src_ref=view(kind, bufs[kind].at[slot], s),
            dst_ref=view(kind, bufs[kind].at[slot], s),
            send_sem=send_sem.at[0],
            recv_sem=sems[kind].at[slot, s],
            device_id=peer(1),
            device_id_type=MESH,
        ).wait_recv()

    stream = [(0, s) for s in range(nq)] + [(1, s) for s in range(nw)]

    def directs(i):
        if i < len(stream):
            kind, s = stream[i]
            for b in bits:
                send(kind, view(kind, shard[kind], s), 2 * b, s, 2 * b)

    def kv_copy(which, d):
        other = lax.rem(c + d, n_c)
        src, dst = ((kc, k_buf), (vc, v_buf))[which]
        return pltpu.make_async_remote_copy(
            src_ref=src.at[:, :, pl.ds(pl.multiple_of(other * kv_cols, LANES), kv_cols)],
            dst_ref=dst.at[pl.ds(c * blk_dev, blk_dev)],
            send_sem=kv_send.at[which, d],
            recv_sem=kv_sem.at[which, d],
            device_id=(f, other),
            device_id_type=MESH,
        )

    directs(0)
    for s in range(nq):
        send(0, view(0, wq, s), 1, s, 1)
    directs(1)

    def tok_copy(j):
        start = pl.multiple_of(flip(j) * depth, LANES)
        return pltpu.make_async_copy(tokens.at[:, pl.ds(start, depth)], tok.at[j], tok_sem.at[j])

    own_q = pltpu.make_async_copy(wq, wq_buf.at[0], own_sem.at[0])
    own_q.start()
    for j in range(n_f):
        tok_copy(j).start()
    kv_sent = []
    for d in range(1, n_c):
        for which in range(2):
            copy = kv_copy(which, d)
            copy.start()
            kv_sent.append(copy)
    mine = pl.ds(pl.multiple_of(c * kv_cols, LANES), kv_cols)
    own_k = pltpu.make_async_copy(kc.at[:, :, mine], k_buf.at[pl.ds(c * blk_dev, blk_dev)], own_sem.at[2])
    own_v = pltpu.make_async_copy(vc.at[:, :, mine], v_buf.at[pl.ds(c * blk_dev, blk_dev)], own_sem.at[3])
    own_k.start()
    own_v.start()

    core = lax.rem(f, 2)
    home = lax.div(f, ratio)
    block = lax.div(lax.rem(f, ratio), 2)

    def move_dst(i, plane):
        return wo_buf.at[
            0,
            pl.ds(pl.multiple_of(plane * part, part), part),
            pl.ds(pl.multiple_of(i * wo_cols, wo_cols), wo_cols),
        ]

    def move(q):
        return pltpu.make_async_remote_copy(
            src_ref=wo.at[pl.ds(pl.multiple_of(q * part, part), part), :],
            dst_ref=move_dst(block, c),
            send_sem=move_send.at[q],
            recv_sem=move_sem.at[block, c],
            device_id=(q * 2 + core, home),
            device_id_type=MESH,
        )

    def keep(q):
        return pltpu.make_async_copy(
            wo.at[pl.ds(pl.multiple_of(q * part, part), part), :], move_dst(block, c), own_sem.at[1]
        )

    def stays(q):
        return jnp.logical_and(home == c, lax.div(f, 2) == q)

    def start_moves():
        @pl.loop(0, chips)
        def _(d):
            q = lax.rem(lax.div(f, 2) + d, chips)

            @pl.when(stays(q))
            def _():
                keep(q).start()

            @pl.when(jnp.logical_not(stays(q)))
            def _():
                move(q).start()

    def wait_moves():
        for i in range(ratio // 2):
            @pl.loop(0, n_c)
            def _(plane):
                own = jnp.logical_and(home == c, jnp.logical_and(plane == c, block == i))

                @pl.when(own)
                def _():
                    keep(lax.div(f, 2)).wait()

                @pl.when(jnp.logical_not(own))
                def _():
                    pltpu.make_async_remote_copy(
                        src_ref=move_dst(i, plane),
                        dst_ref=move_dst(i, plane),
                        send_sem=move_send.at[0],
                        recv_sem=move_sem.at[i, plane],
                        device_id=peer(1),
                        device_id_type=MESH,
                    ).wait_recv()

    acc[...] = jnp.zeros_like(acc)
    tile = min(256, qcols)
    tiles = qcols // tile

    def q_piece(j, s):
        left = tok[j, :, s * qp:(s + 1) * qp]

        @pl.loop(0, tiles)
        def _(t):
            cols = pl.ds(pl.multiple_of(t * tile, tile), tile)
            acc[:, cols] += jnp.dot(
                left, wq_buf[j, s * qp:(s + 1) * qp, cols], preferred_element_type=jnp.float32
            )

    def q_whole(j):
        @pl.loop(0, tiles)
        def _(t):
            cols = pl.ds(pl.multiple_of(t * tile, tile), tile)
            acc[:, cols] += jnp.dot(tok[j], wq_buf[j, :, cols], preferred_element_type=jnp.float32)

    own_q.wait()
    for j in range(n_f):
        tok_copy(j).wait()
    for s in range(nq):
        arrived(0, 1, s)

    @pl.loop(0, 2)
    def _(j):
        q_whole(j)

    def pass_on(i):
        kind, s = stream[i]
        for m in masks:
            arrived(kind, 2 * m, s)
            piece = view(kind, bufs[kind].at[2 * m], s)
            for b in bits:
                if not (m & b) and route(m | b, s) == b:
                    send(kind, piece, 2 * (m | b), s, 2 * b)
            send(kind, piece, 2 * m + 1, s, 1)
            if m == bits[-1] and kind == 0 and i + 2 < nq:
                directs(i + 2)
            if m == bits[-1] and kind == 1:
                directs(i + AHEAD)

    for s in range(nq):
        pass_on(s)
        if s == max(0, nq - 3):
            start_moves()
        if s == nq - 1:
            wait_moves()
            for i in range(AHEAD):
                directs(nq + i)
            for i in range(nw):
                send(1, view(1, shard[1], i), 1, i, 1)

        @pl.loop(2, n_f)
        def _(j):
            @pl.when(lax.rem(j, 2) == 1)
            def _():
                arrived(0, j, s)

            q_piece(j, s)

    for h in range(qcols // HEAD):
        cols = slice(h * HEAD, (h + 1) * HEAD)
        x = acc[:, cols]
        turned = x * cos_ref[...] + pltpu.roll(x, HEAD // 2, 1) * sin_ref[...]
        qc[:, cols] = turned.astype(jnp.bfloat16)

    own_k.wait()
    own_v.wait()
    for copy in kv_sent:
        copy.wait_recv()

    def ctx_copy(b, d):
        q_rows = pl.ds(pl.multiple_of(b * BLOCK, BLOCK), BLOCK)
        return pltpu.make_async_remote_copy(
            src_ref=qc.at[q_rows],
            dst_ref=ctx_all.at[c, q_rows],
            send_sem=ctx_send.at[b, d],
            recv_sem=ctx_sem.at[b, d],
            device_id=(f, lax.rem(c + d, n_c)),
            device_id_type=MESH,
        )

    @pl.loop(0, q_blocks)
    def _(b):
        q_rows = pl.ds(pl.multiple_of(b * BLOCK, BLOCK), BLOCK)
        own_block = n_blocks - q_blocks + b
        later = lax.broadcasted_iota(jnp.int32, (BLOCK, BLOCK), 1) > lax.broadcasted_iota(
            jnp.int32, (BLOCK, BLOCK), 0
        )
        for n in range(n_list):
            entry = lists[0, b, n]
            hide = jnp.where(entry == own_block, -jnp.inf, 0.0)
            bias[:, n * BLOCK:(n + 1) * BLOCK] = jnp.where(later, hide, 0.0)
        for g in range(kv_local):
            head_cols = slice(g * HEAD, (g + 1) * HEAD)
            for n in range(n_list):
                entry = lists[0, b, n]
                k_pick[n * BLOCK:(n + 1) * BLOCK, :] = k_buf[entry, :, head_cols]
                v_pick[n * BLOCK:(n + 1) * BLOCK, :] = v_buf[entry, :, head_cols]
            for i in range(group):
                h = g * group + i
                cols = slice(h * HEAD, (h + 1) * HEAD)
                scores = lax.dot_general(
                    qc[q_rows, cols], k_pick[...], (((1,), (1,)), ((), ())),
                    preferred_element_type=jnp.float32,
                ) + bias[...]
                top = jnp.max(scores, axis=1, keepdims=True)
                raised = jnp.exp(scores - top)
                total = jnp.sum(raised, axis=1, keepdims=True)
                mixed = jnp.dot(
                    raised.astype(jnp.bfloat16), v_pick[...], preferred_element_type=jnp.float32
                )
                qc[q_rows, cols] = (mixed / total).astype(jnp.bfloat16)

        @pl.loop(1, n_c)
        def _(d):
            ctx_copy(b, d).start()

    acc[...] = jnp.zeros_like(acc)

    def share(j, s):
        target = flip(j)
        i, offset = divmod(s * wp, wo_cols)
        start = pl.multiple_of((2 * i + lax.rem(target, 2)) * wo_cols + offset, LANES)
        acc[:, pl.ds(start, wp)] += jnp.dot(
            ctx_perm[lax.div(target, 2)], wo_buf[j, :, s * wp:(s + 1) * wp],
            preferred_element_type=jnp.float32,
        )

    def out_copy(s, k):
        i, offset = divmod(s * wp, wo_cols)
        cols = pl.ds((2 * i + k) * wo_cols + offset, wp)
        return pltpu.make_async_copy(staged.at[:, cols], out.at[:, cols], out_sem.at[s, k])

    for s in range(nw):
        pass_on(nq + s)
    ctx_all[c] = qc[...]

    @pl.loop(0, q_blocks)
    def _(b):
        @pl.loop(1, n_c)
        def _(d):
            ctx_copy(b, d).wait_recv()

    for q in range(chips):
        for plane in range(n_c):
            ctx_perm[q, :, plane * part:(plane + 1) * part] = ctx_all[
                plane, :, q * part:(q + 1) * part
            ]
    for s in range(nw):
        @pl.loop(0, n_f)
        def _(j):
            @pl.when(lax.rem(j, 2) == 1)
            def _():
                arrived(1, j, s)

            share(j, s)

        for k in range(2):
            i, offset = divmod(s * wp, wo_cols)
            cols = pl.ds((2 * i + k) * wo_cols + offset, wp)
            staged[:, cols] = acc[:, cols].astype(jnp.bfloat16)
            out_copy(s, k).start()

    assert len(sent) == send_sem.shape[0]
    for copy in sent + kv_sent:
        copy.wait_send()

    @pl.loop(0, q_blocks)
    def _(b):
        @pl.loop(1, n_c)
        def _(d):
            ctx_copy(b, d).wait_send()

    @pl.loop(0, chips)
    def _(q):
        @pl.when(jnp.logical_not(stays(q)))
        def _():
            move(q).wait_send()

    for s in range(nw):
        for k in range(2):
            out_copy(s, k).wait()


def body(n_f, n_c, tokens, wq, wo, key_cache, value_cache, key_blocks):
    rows, width = tokens.shape
    depth = width // n_f
    qcols = wq.shape[1]
    cache = key_cache.shape[0]
    blk_dev = cache // BLOCK
    kv_cols = key_cache.shape[1] // n_c
    n_list = key_blocks.shape[2]
    cosine, sine = tables(rows, cache * n_c)
    nq = max(1, min(4, wq.shape[0] // LANES))
    ratio = n_f // n_c
    chips = n_f // 2
    part = wo.shape[0] // chips
    moved = (part * n_c, wo.shape[1] * ratio // 2)
    nw = max(1, min(4, moved[1] // LANES))
    any_spec = pl.BlockSpec(memory_space=pl.ANY)
    vmem_spec = pl.BlockSpec(memory_space=pltpu.VMEM)
    bf16 = jnp.bfloat16
    dma = pltpu.SemaphoreType.DMA
    return pl.pallas_call(
        functools.partial(kernel, (n_f, n_c, nq, nw)),
        out_shape=jax.ShapeDtypeStruct((rows, width // n_c), bf16),
        in_specs=[pl.BlockSpec(memory_space=pltpu.SMEM)] + [any_spec] * 5 + [vmem_spec] * 2,
        out_specs=any_spec,
        scratch_shapes=[
            pltpu.VMEM((n_f, rows, depth), bf16),
            pltpu.VMEM((n_f,) + wq.shape, bf16),
            pltpu.VMEM((n_f,) + moved, bf16),
            pltpu.VMEM((blk_dev * n_c, BLOCK, kv_cols), bf16),
            pltpu.VMEM((blk_dev * n_c, BLOCK, kv_cols), bf16),
            pltpu.VMEM((rows, max(qcols, width // n_c)), jnp.float32),
            pltpu.VMEM((rows, qcols), bf16),
            pltpu.VMEM((n_list * BLOCK, HEAD), bf16),
            pltpu.VMEM((n_list * BLOCK, HEAD), bf16),
            pltpu.VMEM((BLOCK, n_list * BLOCK), jnp.float32),
            pltpu.VMEM((n_c, rows, qcols), bf16),
            pltpu.VMEM((chips, rows, n_c * part), bf16),
            pltpu.VMEM((rows, width // n_c), bf16),
            dma((n_f,)),
            dma((4,)),
            dma(((nq + nw) * (n_f - 1),)),
            dma((n_f, nq)),
            dma((n_f, nw)),
            dma((2, n_c)),
            dma((2, n_c)),
            dma((rows // BLOCK, n_c)),
            dma((rows // BLOCK, n_c)),
            dma((chips,)),
            dma((ratio // 2, n_c)),
            dma((nw, 2)),
        ],
        compiler_params=pltpu.CompilerParams(
            collective_id=0, has_side_effects=True, vmem_limit_bytes=67043328
        ),
    )(
        key_blocks,
        tokens,
        wq,
        wo,
        key_cache.reshape(blk_dev, BLOCK, key_cache.shape[1]),
        value_cache.reshape(blk_dev, BLOCK, value_cache.shape[1]),
        cosine,
        sine,
    )


def solution(mesh):
    in_specs = (
        P("fsdp", None),
        P("fsdp", "ctx"),
        P("ctx", "fsdp"),
        P(("fsdp", "ctx"), None),
        P(("fsdp", "ctx"), None),
        P("fsdp", None, None),
    )
    step = functools.partial(body, mesh.shape["fsdp"], mesh.shape["ctx"])
    return jax.shard_map(
        step, mesh=mesh, in_specs=in_specs, out_specs=P("fsdp", "ctx"), check_vma=False
    )
```

```python
import functools

import jax
import jax.numpy as jnp
from jax import lax
from jax.experimental import pallas as pl
from jax.experimental.pallas import tpu as pltpu
from jax.sharding import PartitionSpec as P

HEAD = 128
BLOCK = 128
LANES = 128
AHEAD = 3
MESH = pl.DeviceIdType.MESH

rope_base = 1000000.0


def tables(row_count, key_total):
    half_width = HEAD // 2
    frequency = rope_base ** (-(jnp.arange(half_width, dtype=jnp.float32) * 2.0) / HEAD)
    positions = key_total - row_count + jnp.arange(row_count, dtype=jnp.int32)
    angles = positions.astype(jnp.float32)[:, None] * frequency[None, :]
    cosine = jnp.cos(angles) * HEAD ** (-0.5)
    sine = jnp.sin(angles) * HEAD ** (-0.5)
    return jnp.concatenate([cosine, cosine], axis=1), jnp.concatenate([-sine, sine], axis=1)


def low_bit(m):
    return m & -m


def high_bit(m):
    return 1 << (m.bit_length() - 1)


def route(mask, piece):
    return low_bit(mask) if piece % 2 == 0 else high_bit(mask)


def kernel(
    cfg,
    lists, tokens, wq, wo, kc, vc, cos_ref, sin_ref,
    out,
    tok, wq_buf, wo_buf, k_buf, v_buf, acc, qc, k_pick, v_pick, bias, ctx_all, ctx_perm, staged, hop,
    tok_sem, own_sem, send_sem, wq_sem, wo_sem, kv_send, kv_sem, ctx_send, ctx_sem,
    move_send, move_sem, keep_sem, hop_send, hop_sem, out_sem,
):
    n_f, n_c, nq, nw = cfg
    chips = n_f // 2
    bits = [1 << i for i in range(chips.bit_length() - 1)]
    masks = sorted(range(1, chips), key=lambda m: (bin(m).count("1"), m))
    f = lax.axis_index("fsdp")
    c = lax.axis_index("ctx")
    rows = tok.shape[1]
    depth = tok.shape[2]
    qcols = wq_buf.shape[2]
    qp = wq_buf.shape[1] // nq
    wo_cols = wo.shape[1]
    wp = wo_buf.shape[2] // nw
    part = wo.shape[0] // chips
    ratio = n_f // n_c
    blk_dev = kc.shape[0]
    kv_cols = k_buf.shape[2]
    kv_local = kv_cols // HEAD
    group = qcols // kv_cols
    n_blocks = k_buf.shape[0]
    q_blocks = rows // BLOCK
    n_list = lists.shape[2]

    def flip(x):
        bit, total = 1, 0
        while bit < n_f:
            total += lax.rem(lax.div(f, bit) + x // bit, 2) * bit
            bit *= 2
        return total

    def peer(x):
        return (flip(x), c)

    barrier = pltpu.get_barrier_semaphore()
    me = f * n_c + c

    @pl.loop(1, n_f * n_c)
    def _(d):
        other = lax.rem(me + d, n_f * n_c)
        pl.semaphore_signal(
            barrier, inc=1, device_id=(lax.div(other, n_c), lax.rem(other, n_c)), device_id_type=MESH
        )

    pl.semaphore_wait(barrier, n_f * n_c - 1)

    sent = []

    def view(kind, ref, s):
        if kind == 0:
            return ref.at[pl.ds(s * qp, qp), :]
        return ref.at[:, pl.ds(s * wp, wp)]

    shard = (wq, wo_buf.at[0])
    bufs = (wq_buf, wo_buf)
    sems = (wq_sem, wo_sem)
    counts = (nq, nw)

    def send(kind, src, slot, s, to):
        copy = pltpu.make_async_remote_copy(
            src_ref=src,
            dst_ref=view(kind, bufs[kind].at[slot], s),
            send_sem=send_sem.at[len(sent)],
            recv_sem=sems[kind].at[slot, s],
            device_id=peer(to),
            device_id_type=MESH,
        )
        copy.start()
        sent.append(copy)

    def arrived(kind, slot, s):
        pltpu.make_async_remote_copy(
            src_ref=view(kind, bufs[kind].at[slot], s),
            dst_ref=view(kind, bufs[kind].at[slot], s),
            send_sem=send_sem.at[0],
            recv_sem=sems[kind].at[slot, s],
            device_id=peer(1),
            device_id_type=MESH,
        ).wait_recv()

    stream = [(0, s) for s in range(nq)] + [(1, s) for s in range(nw)]

    def directs(i):
        if i < len(stream):
            kind, s = stream[i]
            for b in bits:
                send(kind, view(kind, shard[kind], s), 2 * b, s, 2 * b)

    def kv_copy(which, d):
        other = lax.rem(c + d, n_c)
        src, dst = ((kc, k_buf), (vc, v_buf))[which]
        return pltpu.make_async_remote_copy(
            src_ref=src.at[:, :, pl.ds(pl.multiple_of(other * kv_cols, LANES), kv_cols)],
            dst_ref=dst.at[pl.ds(c * blk_dev, blk_dev)],
            send_sem=kv_send.at[which, d],
            recv_sem=kv_sem.at[which, d],
            device_id=(f, other),
            device_id_type=MESH,
        )

    core = lax.rem(f, 2)
    chip = lax.div(f, 2)

    def piece(q):
        return wo.at[pl.ds(pl.multiple_of(q * part, part), part), :]

    def hop_copy(q, source):
        return pltpu.make_async_remote_copy(
            src_ref=piece(q),
            dst_ref=hop.at[source],
            send_sem=hop_send.at[q],
            recv_sem=hop_sem.at[source],
            device_id=(q * 2 + core, c),
            device_id_type=MESH,
        )

    def move_dst(i, plane):
        return wo_buf.at[
            0,
            pl.ds(pl.multiple_of(plane * part, part), part),
            pl.ds(pl.multiple_of(i * wo_cols, wo_cols), wo_cols),
        ]

    def owner(p):
        source = p * 2 + core
        return lax.div(source, ratio), lax.div(lax.rem(source, ratio), 2)

    def move(src, p):
        home, i = owner(p)
        return pltpu.make_async_remote_copy(
            src_ref=src,
            dst_ref=move_dst(i, c),
            send_sem=move_send.at[p],
            recv_sem=move_sem.at[i, c],
            device_id=(f, home),
            device_id_type=MESH,
        )

    def keep(src, p):
        _, i = owner(p)
        return pltpu.make_async_copy(src, move_dst(i, c), keep_sem.at[i])

    def start_hops():
        @pl.loop(1, chips)
        def _(d):
            hop_copy(lax.rem(chip + d, chips), chip).start()

    def forward(src, p):
        home, _ = owner(p)

        @pl.when(home == c)
        def _():
            keep(src, p).start()

        @pl.when(home != c)
        def _():
            move(src, p).start()

    def start_moves():
        forward(piece(chip), chip)

        @pl.loop(1, chips)
        def _(d):
            p = lax.rem(chip + d, chips)
            hop_copy(p, p).wait_recv()
            forward(hop.at[p], p)

    def wait_moves():
        for i in range(ratio // 2):
            keep(piece(chip), lax.div(c * ratio + 2 * i, 2)).wait()

            @pl.loop(1, n_c)
            def _(d):
                plane = lax.rem(c + d, n_c)
                pltpu.make_async_remote_copy(
                    src_ref=move_dst(i, plane),
                    dst_ref=move_dst(i, plane),
                    send_sem=move_send.at[0],
                    recv_sem=move_sem.at[i, plane],
                    device_id=peer(1),
                    device_id_type=MESH,
                ).wait_recv()

    start_hops()
    directs(0)
    for s in range(nq):
        send(0, view(0, wq, s), 1, s, 1)
    directs(1)

    def tok_copy(j):
        start = pl.multiple_of(flip(j) * depth, LANES)
        return pltpu.make_async_copy(tokens.at[:, pl.ds(start, depth)], tok.at[j], tok_sem.at[j])

    own_q = pltpu.make_async_copy(wq, wq_buf.at[0], own_sem.at[0])
    own_q.start()
    for j in range(n_f):
        tok_copy(j).start()
    kv_sent = []
    for d in range(1, n_c):
        for which in range(2):
            copy = kv_copy(which, d)
            copy.start()
            kv_sent.append(copy)
    mine = pl.ds(pl.multiple_of(c * kv_cols, LANES), kv_cols)
    own_k = pltpu.make_async_copy(kc.at[:, :, mine], k_buf.at[pl.ds(c * blk_dev, blk_dev)], own_sem.at[2])
    own_v = pltpu.make_async_copy(vc.at[:, :, mine], v_buf.at[pl.ds(c * blk_dev, blk_dev)], own_sem.at[3])
    own_k.start()
    own_v.start()

    acc[...] = jnp.zeros_like(acc)
    tile = min(256, qcols)
    tiles = qcols // tile

    def q_piece(j, s):
        left = tok[j, :, s * qp:(s + 1) * qp]

        @pl.loop(0, tiles)
        def _(t):
            cols = pl.ds(pl.multiple_of(t * tile, tile), tile)
            acc[:, cols] += jnp.dot(
                left, wq_buf[j, s * qp:(s + 1) * qp, cols], preferred_element_type=jnp.float32
            )

    def q_whole(j):
        @pl.loop(0, tiles)
        def _(t):
            cols = pl.ds(pl.multiple_of(t * tile, tile), tile)
            acc[:, cols] += jnp.dot(tok[j], wq_buf[j, :, cols], preferred_element_type=jnp.float32)

    own_q.wait()
    for j in range(n_f):
        tok_copy(j).wait()
    for s in range(nq):
        arrived(0, 1, s)

    @pl.loop(0, 2)
    def _(j):
        q_whole(j)

    def pass_on(i):
        kind, s = stream[i]
        for m in masks:
            arrived(kind, 2 * m, s)
            piece = view(kind, bufs[kind].at[2 * m], s)
            for b in bits:
                if not (m & b) and route(m | b, s) == b:
                    send(kind, piece, 2 * (m | b), s, 2 * b)
            send(kind, piece, 2 * m + 1, s, 1)
            if m == bits[-1] and kind == 0 and i + 2 < nq:
                directs(i + 2)
            if m == bits[-1] and kind == 1:
                directs(i + AHEAD)

    for s in range(nq):
        pass_on(s)
        if s == 0:
            start_moves()
        if s == max(0, nq - 2):
            wait_moves()
            directs(nq)
            for i in range(nw):
                send(1, view(1, shard[1], i), 1, i, 1)
        if s == nq - 1:
            for i in range(1, AHEAD):
                directs(nq + i)

        @pl.loop(2, n_f)
        def _(j):
            @pl.when(lax.rem(j, 2) == 1)
            def _():
                arrived(0, j, s)

            q_piece(j, s)

    for h in range(qcols // HEAD):
        cols = slice(h * HEAD, (h + 1) * HEAD)
        x = acc[:, cols]
        turned = x * cos_ref[...] + pltpu.roll(x, HEAD // 2, 1) * sin_ref[...]
        qc[:, cols] = turned.astype(jnp.bfloat16)

    own_k.wait()
    own_v.wait()
    for copy in kv_sent:
        copy.wait_recv()

    def ctx_copy(b, d):
        q_rows = pl.ds(pl.multiple_of(b * BLOCK, BLOCK), BLOCK)
        return pltpu.make_async_remote_copy(
            src_ref=qc.at[q_rows],
            dst_ref=ctx_all.at[c, q_rows],
            send_sem=ctx_send.at[b, d],
            recv_sem=ctx_sem.at[b, d],
            device_id=(f, lax.rem(c + d, n_c)),
            device_id_type=MESH,
        )

    @pl.loop(0, q_blocks)
    def _(b):
        q_rows = pl.ds(pl.multiple_of(b * BLOCK, BLOCK), BLOCK)
        own_block = n_blocks - q_blocks + b
        later = lax.broadcasted_iota(jnp.int32, (BLOCK, BLOCK), 1) > lax.broadcasted_iota(
            jnp.int32, (BLOCK, BLOCK), 0
        )
        for n in range(n_list):
            entry = lists[0, b, n]
            hide = jnp.where(entry == own_block, -jnp.inf, 0.0)
            bias[:, n * BLOCK:(n + 1) * BLOCK] = jnp.where(later, hide, 0.0)
        for g in range(kv_local):
            head_cols = slice(g * HEAD, (g + 1) * HEAD)
            for n in range(n_list):
                entry = lists[0, b, n]
                k_pick[n * BLOCK:(n + 1) * BLOCK, :] = k_buf[entry, :, head_cols]
                v_pick[n * BLOCK:(n + 1) * BLOCK, :] = v_buf[entry, :, head_cols]
            for i in range(group):
                h = g * group + i
                cols = slice(h * HEAD, (h + 1) * HEAD)
                scores = lax.dot_general(
                    qc[q_rows, cols], k_pick[...], (((1,), (1,)), ((), ())),
                    preferred_element_type=jnp.float32,
                ) + bias[...]
                top = jnp.max(scores, axis=1, keepdims=True)
                raised = jnp.exp(scores - top)
                total = jnp.sum(raised, axis=1, keepdims=True)
                mixed = jnp.dot(
                    raised.astype(jnp.bfloat16), v_pick[...], preferred_element_type=jnp.float32
                )
                qc[q_rows, cols] = (mixed / total).astype(jnp.bfloat16)

        @pl.loop(1, n_c)
        def _(d):
            ctx_copy(b, d).start()

    acc[...] = jnp.zeros_like(acc)

    def share(j, s):
        target = flip(j)
        i, offset = divmod(s * wp, wo_cols)
        start = pl.multiple_of((2 * i + lax.rem(target, 2)) * wo_cols + offset, LANES)
        acc[:, pl.ds(start, wp)] += jnp.dot(
            ctx_perm[lax.div(target, 2)], wo_buf[j, :, s * wp:(s + 1) * wp],
            preferred_element_type=jnp.float32,
        )

    def out_copy(s, k):
        i, offset = divmod(s * wp, wo_cols)
        cols = pl.ds((2 * i + k) * wo_cols + offset, wp)
        return pltpu.make_async_copy(staged.at[:, cols], out.at[:, cols], out_sem.at[s, k])

    for s in range(nw):
        pass_on(nq + s)
    ctx_all[c] = qc[...]

    @pl.loop(0, q_blocks)
    def _(b):
        @pl.loop(1, n_c)
        def _(d):
            ctx_copy(b, d).wait_recv()

    for q in range(chips):
        for plane in range(n_c):
            ctx_perm[q, :, plane * part:(plane + 1) * part] = ctx_all[
                plane, :, q * part:(q + 1) * part
            ]
    for s in range(nw):
        @pl.loop(0, n_f)
        def _(j):
            @pl.when(lax.rem(j, 2) == 1)
            def _():
                arrived(1, j, s)

            share(j, s)

        for k in range(2):
            i, offset = divmod(s * wp, wo_cols)
            cols = pl.ds((2 * i + k) * wo_cols + offset, wp)
            staged[:, cols] = acc[:, cols].astype(jnp.bfloat16)
            out_copy(s, k).start()

    assert len(sent) == send_sem.shape[0]
    for copy in sent + kv_sent:
        copy.wait_send()

    @pl.loop(0, q_blocks)
    def _(b):
        @pl.loop(1, n_c)
        def _(d):
            ctx_copy(b, d).wait_send()

    @pl.loop(0, chips)
    def _(q):
        @pl.when(q != chip)
        def _():
            hop_copy(q, chip).wait_send()

        home, _ = owner(q)

        @pl.when(home != c)
        def _():
            move(piece(chip), q).wait_send()

    for s in range(nw):
        for k in range(2):
            out_copy(s, k).wait()


def body(n_f, n_c, tokens, wq, wo, key_cache, value_cache, key_blocks):
    rows, width = tokens.shape
    depth = width // n_f
    qcols = wq.shape[1]
    cache = key_cache.shape[0]
    blk_dev = cache // BLOCK
    kv_cols = key_cache.shape[1] // n_c
    n_list = key_blocks.shape[2]
    cosine, sine = tables(rows, cache * n_c)
    nq = max(1, min(4, wq.shape[0] // LANES))
    ratio = n_f // n_c
    chips = n_f // 2
    part = wo.shape[0] // chips
    moved = (part * n_c, wo.shape[1] * ratio // 2)
    nw = max(1, min(4, moved[1] // LANES))
    any_spec = pl.BlockSpec(memory_space=pl.ANY)
    vmem_spec = pl.BlockSpec(memory_space=pltpu.VMEM)
    bf16 = jnp.bfloat16
    dma = pltpu.SemaphoreType.DMA
    return pl.pallas_call(
        functools.partial(kernel, (n_f, n_c, nq, nw)),
        out_shape=jax.ShapeDtypeStruct((rows, width // n_c), bf16),
        in_specs=[pl.BlockSpec(memory_space=pltpu.SMEM)] + [any_spec] * 5 + [vmem_spec] * 2,
        out_specs=any_spec,
        scratch_shapes=[
            pltpu.VMEM((n_f, rows, depth), bf16),
            pltpu.VMEM((n_f,) + wq.shape, bf16),
            pltpu.VMEM((n_f,) + moved, bf16),
            pltpu.VMEM((blk_dev * n_c, BLOCK, kv_cols), bf16),
            pltpu.VMEM((blk_dev * n_c, BLOCK, kv_cols), bf16),
            pltpu.VMEM((rows, max(qcols, width // n_c)), jnp.float32),
            pltpu.VMEM((rows, qcols), bf16),
            pltpu.VMEM((n_list * BLOCK, HEAD), bf16),
            pltpu.VMEM((n_list * BLOCK, HEAD), bf16),
            pltpu.VMEM((BLOCK, n_list * BLOCK), jnp.float32),
            pltpu.VMEM((n_c, rows, qcols), bf16),
            pltpu.VMEM((chips, rows, n_c * part), bf16),
            pltpu.VMEM((rows, width // n_c), bf16),
            pltpu.VMEM((chips, part, wo.shape[1]), bf16),
            dma((n_f,)),
            dma((4,)),
            dma(((nq + nw) * (n_f - 1),)),
            dma((n_f, nq)),
            dma((n_f, nw)),
            dma((2, n_c)),
            dma((2, n_c)),
            dma((rows // BLOCK, n_c)),
            dma((rows // BLOCK, n_c)),
            dma((chips,)),
            dma((ratio // 2, n_c)),
            dma((ratio // 2,)),
            dma((chips,)),
            dma((chips,)),
            dma((nw, 2)),
        ],
        compiler_params=pltpu.CompilerParams(
            collective_id=0, has_side_effects=True, vmem_limit_bytes=67043328
        ),
    )(
        key_blocks,
        tokens,
        wq,
        wo,
        key_cache.reshape(blk_dev, BLOCK, key_cache.shape[1]),
        value_cache.reshape(blk_dev, BLOCK, value_cache.shape[1]),
        cosine,
        sine,
    )


def solution(mesh):
    in_specs = (
        P("fsdp", None),
        P("fsdp", "ctx"),
        P("ctx", "fsdp"),
        P(("fsdp", "ctx"), None),
        P(("fsdp", "ctx"), None),
        P("fsdp", None, None),
    )
    step = functools.partial(body, mesh.shape["fsdp"], mesh.shape["ctx"])
    return jax.shard_map(
        step, mesh=mesh, in_specs=in_specs, out_specs=P("fsdp", "ctx"), check_vma=False
    )
```

```python
import functools

import jax
import jax.numpy as jnp
from jax import lax
from jax.experimental import pallas as pl
from jax.experimental.pallas import tpu as pltpu
from jax.sharding import PartitionSpec as P

HEAD = 128
BLOCK = 128
LANES = 128
AHEAD = 4
MESH = pl.DeviceIdType.MESH

rope_base = 1000000.0


def tables(row_count, key_total):
    half_width = HEAD // 2
    frequency = rope_base ** (-(jnp.arange(half_width, dtype=jnp.float32) * 2.0) / HEAD)
    positions = key_total - row_count + jnp.arange(row_count, dtype=jnp.int32)
    angles = positions.astype(jnp.float32)[:, None] * frequency[None, :]
    cosine = jnp.cos(angles) * HEAD ** (-0.5)
    sine = jnp.sin(angles) * HEAD ** (-0.5)
    return jnp.concatenate([cosine, cosine], axis=1), jnp.concatenate([-sine, sine], axis=1)


def low_bit(m):
    return m & -m


def high_bit(m):
    return 1 << (m.bit_length() - 1)


def route(mask, piece):
    return low_bit(mask) if piece % 2 == 0 else high_bit(mask)


def kernel(
    cfg,
    lists, tokens, wq, wo, kc, vc, cos_ref, sin_ref,
    out,
    tok, wq_buf, wo_buf, k_buf, v_buf, acc, qc, k_pick, v_pick, bias, ctx_all, ctx_perm, staged, hop,
    tok_sem, own_sem, send_sem, wq_sem, wo_sem, kv_send, kv_sem, ctx_send, ctx_sem,
    move_send, move_sem, keep_sem, hop_send, hop_sem, out_sem,
):
    n_f, n_c, nq, nw = cfg
    chips = n_f // 2
    bits = [1 << i for i in range(chips.bit_length() - 1)]
    masks = sorted(range(1, chips), key=lambda m: (bin(m).count("1"), m))
    f = lax.axis_index("fsdp")
    c = lax.axis_index("ctx")
    rows = tok.shape[1]
    depth = tok.shape[2]
    qcols = wq_buf.shape[2]
    qp = wq_buf.shape[1] // nq
    wo_cols = wo.shape[1]
    wp = wo_buf.shape[2] // nw
    part = wo.shape[0] // chips
    ratio = n_f // n_c
    blk_dev = kc.shape[0]
    kv_cols = k_buf.shape[2]
    kv_local = kv_cols // HEAD
    group = qcols // kv_cols
    n_blocks = k_buf.shape[0]
    q_blocks = rows // BLOCK
    n_list = lists.shape[2]

    def flip(x):
        bit, total = 1, 0
        while bit < n_f:
            total += lax.rem(lax.div(f, bit) + x // bit, 2) * bit
            bit *= 2
        return total

    def peer(x):
        return (flip(x), c)

    barrier = pltpu.get_barrier_semaphore()
    me = f * n_c + c

    @pl.loop(1, n_f * n_c)
    def _(d):
        other = lax.rem(me + d, n_f * n_c)
        pl.semaphore_signal(
            barrier, inc=1, device_id=(lax.div(other, n_c), lax.rem(other, n_c)), device_id_type=MESH
        )

    pl.semaphore_wait(barrier, n_f * n_c - 1)

    sent = []

    def view(kind, ref, s):
        if kind == 0:
            return ref.at[pl.ds(s * qp, qp), :]
        return ref.at[:, pl.ds(s * wp, wp)]

    shard = (wq, wo_buf.at[0])
    bufs = (wq_buf, wo_buf)
    sems = (wq_sem, wo_sem)
    counts = (nq, nw)

    def send(kind, src, slot, s, to):
        copy = pltpu.make_async_remote_copy(
            src_ref=src,
            dst_ref=view(kind, bufs[kind].at[slot], s),
            send_sem=send_sem.at[len(sent)],
            recv_sem=sems[kind].at[slot, s],
            device_id=peer(to),
            device_id_type=MESH,
        )
        copy.start()
        sent.append(copy)

    def arrived(kind, slot, s):
        pltpu.make_async_remote_copy(
            src_ref=view(kind, bufs[kind].at[slot], s),
            dst_ref=view(kind, bufs[kind].at[slot], s),
            send_sem=send_sem.at[0],
            recv_sem=sems[kind].at[slot, s],
            device_id=peer(1),
            device_id_type=MESH,
        ).wait_recv()

    stream = [(0, s) for s in range(nq)] + [(1, s) for s in range(nw)]

    def directs(i):
        if i < len(stream):
            kind, s = stream[i]
            for b in bits:
                send(kind, view(kind, shard[kind], s), 2 * b, s, 2 * b)

    def kv_copy(which, d):
        other = lax.rem(c + d, n_c)
        src, dst = ((kc, k_buf), (vc, v_buf))[which]
        return pltpu.make_async_remote_copy(
            src_ref=src.at[:, :, pl.ds(pl.multiple_of(other * kv_cols, LANES), kv_cols)],
            dst_ref=dst.at[pl.ds(c * blk_dev, blk_dev)],
            send_sem=kv_send.at[which, d],
            recv_sem=kv_sem.at[which, d],
            device_id=(f, other),
            device_id_type=MESH,
        )

    core = lax.rem(f, 2)
    chip = lax.div(f, 2)

    def piece(q):
        return wo.at[pl.ds(pl.multiple_of(q * part, part), part), :]

    def hop_copy(q, source):
        return pltpu.make_async_remote_copy(
            src_ref=piece(q),
            dst_ref=hop.at[source],
            send_sem=hop_send.at[q],
            recv_sem=hop_sem.at[source],
            device_id=(q * 2 + core, c),
            device_id_type=MESH,
        )

    def move_dst(i, plane):
        return wo_buf.at[
            0,
            pl.ds(pl.multiple_of(plane * part, part), part),
            pl.ds(pl.multiple_of(i * wo_cols, wo_cols), wo_cols),
        ]

    def owner(p):
        source = p * 2 + core
        return lax.div(source, ratio), lax.div(lax.rem(source, ratio), 2)

    def move(src, p):
        home, i = owner(p)
        return pltpu.make_async_remote_copy(
            src_ref=src,
            dst_ref=move_dst(i, c),
            send_sem=move_send.at[p],
            recv_sem=move_sem.at[i, c],
            device_id=(f, home),
            device_id_type=MESH,
        )

    def keep(src, p):
        _, i = owner(p)
        return pltpu.make_async_copy(src, move_dst(i, c), keep_sem.at[i])

    def start_hops():
        @pl.loop(1, chips)
        def _(d):
            hop_copy(lax.rem(chip + d, chips), chip).start()

    def forward(src, p):
        home, _ = owner(p)

        @pl.when(home == c)
        def _():
            keep(src, p).start()

        @pl.when(home != c)
        def _():
            move(src, p).start()

    def start_moves():
        forward(piece(chip), chip)

        @pl.loop(1, chips)
        def _(d):
            p = lax.rem(chip + d, chips)
            hop_copy(p, p).wait_recv()
            forward(hop.at[p], p)

    def wait_moves():
        for i in range(ratio // 2):
            keep(piece(chip), lax.div(c * ratio + 2 * i, 2)).wait()

            @pl.loop(1, n_c)
            def _(d):
                plane = lax.rem(c + d, n_c)
                pltpu.make_async_remote_copy(
                    src_ref=move_dst(i, plane),
                    dst_ref=move_dst(i, plane),
                    send_sem=move_send.at[0],
                    recv_sem=move_sem.at[i, plane],
                    device_id=peer(1),
                    device_id_type=MESH,
                ).wait_recv()

    start_hops()
    directs(0)
    for s in range(nq):
        send(0, view(0, wq, s), 1, s, 1)
    directs(1)

    def tok_copy(j):
        start = pl.multiple_of(flip(j) * depth, LANES)
        return pltpu.make_async_copy(tokens.at[:, pl.ds(start, depth)], tok.at[j], tok_sem.at[j])

    own_q = pltpu.make_async_copy(wq, wq_buf.at[0], own_sem.at[0])
    own_q.start()
    for j in range(n_f):
        tok_copy(j).start()
    kv_sent = []
    for d in range(1, n_c):
        for which in range(2):
            copy = kv_copy(which, d)
            copy.start()
            kv_sent.append(copy)
    mine = pl.ds(pl.multiple_of(c * kv_cols, LANES), kv_cols)
    own_k = pltpu.make_async_copy(kc.at[:, :, mine], k_buf.at[pl.ds(c * blk_dev, blk_dev)], own_sem.at[2])
    own_v = pltpu.make_async_copy(vc.at[:, :, mine], v_buf.at[pl.ds(c * blk_dev, blk_dev)], own_sem.at[3])
    own_k.start()
    own_v.start()

    acc[...] = jnp.zeros_like(acc)
    tile = min(256, qcols)
    tiles = qcols // tile

    def q_piece(j, s):
        left = tok[j, :, s * qp:(s + 1) * qp]

        @pl.loop(0, tiles)
        def _(t):
            cols = pl.ds(pl.multiple_of(t * tile, tile), tile)
            acc[:, cols] += jnp.dot(
                left, wq_buf[j, s * qp:(s + 1) * qp, cols], preferred_element_type=jnp.float32
            )

    def q_whole(j):
        @pl.loop(0, tiles)
        def _(t):
            cols = pl.ds(pl.multiple_of(t * tile, tile), tile)
            acc[:, cols] += jnp.dot(tok[j], wq_buf[j, :, cols], preferred_element_type=jnp.float32)

    own_q.wait()
    for j in range(n_f):
        tok_copy(j).wait()
    for s in range(nq):
        arrived(0, 1, s)

    @pl.loop(0, 2)
    def _(j):
        q_whole(j)

    def pass_on(i):
        kind, s = stream[i]
        for m in masks:
            arrived(kind, 2 * m, s)
            piece = view(kind, bufs[kind].at[2 * m], s)
            for b in bits:
                if not (m & b) and route(m | b, s) == b:
                    send(kind, piece, 2 * (m | b), s, 2 * b)
            send(kind, piece, 2 * m + 1, s, 1)
            if m == bits[-1] and kind == 0 and i + 2 < nq:
                directs(i + 2)
            if m == bits[-1] and kind == 1:
                directs(i + AHEAD)

    for s in range(nq):
        pass_on(s)
        if s == 0:
            start_moves()
        if s == max(0, nq - 2):
            wait_moves()
            directs(nq)
            for i in range(nw):
                send(1, view(1, shard[1], i), 1, i, 1)
        if s == nq - 1:
            for i in range(1, AHEAD):
                directs(nq + i)

        @pl.loop(2, n_f)
        def _(j):
            @pl.when(lax.rem(j, 2) == 1)
            def _():
                arrived(0, j, s)

            q_piece(j, s)

    for h in range(qcols // HEAD):
        cols = slice(h * HEAD, (h + 1) * HEAD)
        x = acc[:, cols]
        turned = x * cos_ref[...] + pltpu.roll(x, HEAD // 2, 1) * sin_ref[...]
        qc[:, cols] = turned.astype(jnp.bfloat16)

    own_k.wait()
    own_v.wait()
    for copy in kv_sent:
        copy.wait_recv()

    def ctx_copy(b, d):
        q_rows = pl.ds(pl.multiple_of(b * BLOCK, BLOCK), BLOCK)
        return pltpu.make_async_remote_copy(
            src_ref=qc.at[q_rows],
            dst_ref=ctx_all.at[c, q_rows],
            send_sem=ctx_send.at[b, d],
            recv_sem=ctx_sem.at[b, d],
            device_id=(f, lax.rem(c + d, n_c)),
            device_id_type=MESH,
        )

    @pl.loop(0, q_blocks)
    def _(b):
        q_rows = pl.ds(pl.multiple_of(b * BLOCK, BLOCK), BLOCK)
        own_block = n_blocks - q_blocks + b
        later = lax.broadcasted_iota(jnp.int32, (BLOCK, BLOCK), 1) > lax.broadcasted_iota(
            jnp.int32, (BLOCK, BLOCK), 0
        )
        for n in range(n_list):
            entry = lists[0, b, n]
            hide = jnp.where(entry == own_block, -jnp.inf, 0.0)
            bias[:, n * BLOCK:(n + 1) * BLOCK] = jnp.where(later, hide, 0.0)
        for g in range(kv_local):
            head_cols = slice(g * HEAD, (g + 1) * HEAD)
            for n in range(n_list):
                entry = lists[0, b, n]
                k_pick[n * BLOCK:(n + 1) * BLOCK, :] = k_buf[entry, :, head_cols]
                v_pick[n * BLOCK:(n + 1) * BLOCK, :] = v_buf[entry, :, head_cols]
            for i in range(group):
                h = g * group + i
                cols = slice(h * HEAD, (h + 1) * HEAD)
                scores = lax.dot_general(
                    qc[q_rows, cols], k_pick[...], (((1,), (1,)), ((), ())),
                    preferred_element_type=jnp.float32,
                ) + bias[...]
                top = jnp.max(scores, axis=1, keepdims=True)
                raised = jnp.exp(scores - top)
                total = jnp.sum(raised, axis=1, keepdims=True)
                mixed = jnp.dot(
                    raised.astype(jnp.bfloat16), v_pick[...], preferred_element_type=jnp.float32
                )
                qc[q_rows, cols] = (mixed / total).astype(jnp.bfloat16)

        @pl.loop(1, n_c)
        def _(d):
            ctx_copy(b, d).start()

    acc[...] = jnp.zeros_like(acc)

    def share(j, s):
        target = flip(j)
        i, offset = divmod(s * wp, wo_cols)
        start = pl.multiple_of((2 * i + lax.rem(target, 2)) * wo_cols + offset, LANES)
        acc[:, pl.ds(start, wp)] += jnp.dot(
            ctx_perm[lax.div(target, 2)], wo_buf[j, :, s * wp:(s + 1) * wp],
            preferred_element_type=jnp.float32,
        )

    def out_copy(s, k):
        i, offset = divmod(s * wp, wo_cols)
        cols = pl.ds((2 * i + k) * wo_cols + offset, wp)
        return pltpu.make_async_copy(staged.at[:, cols], out.at[:, cols], out_sem.at[s, k])

    for s in range(nw):
        pass_on(nq + s)
    ctx_all[c] = qc[...]

    @pl.loop(0, q_blocks)
    def _(b):
        @pl.loop(1, n_c)
        def _(d):
            ctx_copy(b, d).wait_recv()

    for q in range(chips):
        for plane in range(n_c):
            ctx_perm[q, :, plane * part:(plane + 1) * part] = ctx_all[
                plane, :, q * part:(q + 1) * part
            ]
    for s in range(nw):
        @pl.loop(0, n_f)
        def _(j):
            @pl.when(lax.rem(j, 2) == 1)
            def _():
                arrived(1, j, s)

            share(j, s)

        for k in range(2):
            i, offset = divmod(s * wp, wo_cols)
            cols = pl.ds((2 * i + k) * wo_cols + offset, wp)
            staged[:, cols] = acc[:, cols].astype(jnp.bfloat16)
            out_copy(s, k).start()

    assert len(sent) == send_sem.shape[0]
    for copy in sent + kv_sent:
        copy.wait_send()

    @pl.loop(0, q_blocks)
    def _(b):
        @pl.loop(1, n_c)
        def _(d):
            ctx_copy(b, d).wait_send()

    @pl.loop(0, chips)
    def _(q):
        @pl.when(q != chip)
        def _():
            hop_copy(q, chip).wait_send()

        home, _ = owner(q)

        @pl.when(home != c)
        def _():
            move(piece(chip), q).wait_send()

    for s in range(nw):
        for k in range(2):
            out_copy(s, k).wait()


def body(n_f, n_c, tokens, wq, wo, key_cache, value_cache, key_blocks):
    rows, width = tokens.shape
    depth = width // n_f
    qcols = wq.shape[1]
    cache = key_cache.shape[0]
    blk_dev = cache // BLOCK
    kv_cols = key_cache.shape[1] // n_c
    n_list = key_blocks.shape[2]
    cosine, sine = tables(rows, cache * n_c)
    nq = max(1, min(4, wq.shape[0] // LANES))
    ratio = n_f // n_c
    chips = n_f // 2
    part = wo.shape[0] // chips
    moved = (part * n_c, wo.shape[1] * ratio // 2)
    nw = max(1, min(4, moved[1] // LANES))
    any_spec = pl.BlockSpec(memory_space=pl.ANY)
    vmem_spec = pl.BlockSpec(memory_space=pltpu.VMEM)
    bf16 = jnp.bfloat16
    dma = pltpu.SemaphoreType.DMA
    return pl.pallas_call(
        functools.partial(kernel, (n_f, n_c, nq, nw)),
        out_shape=jax.ShapeDtypeStruct((rows, width // n_c), bf16),
        in_specs=[pl.BlockSpec(memory_space=pltpu.SMEM)] + [any_spec] * 5 + [vmem_spec] * 2,
        out_specs=any_spec,
        scratch_shapes=[
            pltpu.VMEM((n_f, rows, depth), bf16),
            pltpu.VMEM((n_f,) + wq.shape, bf16),
            pltpu.VMEM((n_f,) + moved, bf16),
            pltpu.VMEM((blk_dev * n_c, BLOCK, kv_cols), bf16),
            pltpu.VMEM((blk_dev * n_c, BLOCK, kv_cols), bf16),
            pltpu.VMEM((rows, max(qcols, width // n_c)), jnp.float32),
            pltpu.VMEM((rows, qcols), bf16),
            pltpu.VMEM((n_list * BLOCK, HEAD), bf16),
            pltpu.VMEM((n_list * BLOCK, HEAD), bf16),
            pltpu.VMEM((BLOCK, n_list * BLOCK), jnp.float32),
            pltpu.VMEM((n_c, rows, qcols), bf16),
            pltpu.VMEM((chips, rows, n_c * part), bf16),
            pltpu.VMEM((rows, width // n_c), bf16),
            pltpu.VMEM((chips, part, wo.shape[1]), bf16),
            dma((n_f,)),
            dma((4,)),
            dma(((nq + nw) * (n_f - 1),)),
            dma((n_f, nq)),
            dma((n_f, nw)),
            dma((2, n_c)),
            dma((2, n_c)),
            dma((rows // BLOCK, n_c)),
            dma((rows // BLOCK, n_c)),
            dma((chips,)),
            dma((ratio // 2, n_c)),
            dma((ratio // 2,)),
            dma((chips,)),
            dma((chips,)),
            dma((nw, 2)),
        ],
        compiler_params=pltpu.CompilerParams(
            collective_id=0, has_side_effects=True, vmem_limit_bytes=67043328
        ),
    )(
        key_blocks,
        tokens,
        wq,
        wo,
        key_cache.reshape(blk_dev, BLOCK, key_cache.shape[1]),
        value_cache.reshape(blk_dev, BLOCK, value_cache.shape[1]),
        cosine,
        sine,
    )


def solution(mesh):
    in_specs = (
        P("fsdp", None),
        P("fsdp", "ctx"),
        P("ctx", "fsdp"),
        P(("fsdp", "ctx"), None),
        P(("fsdp", "ctx"), None),
        P("fsdp", None, None),
    )
    step = functools.partial(body, mesh.shape["fsdp"], mesh.shape["ctx"])
    return jax.shard_map(
        step, mesh=mesh, in_specs=in_specs, out_specs=P("fsdp", "ctx"), check_vma=False
    )
```
